32 devices in a mesh: views: 2 (over x), depth: 2 (over core), lat: 8 (over z, y).
Axes of the slice: x: 2, y: 2, z: 4, core: 2. Of those that a mesh axis runs over, the one named last changes fastest.
Arguments:
- volume: bfloat16 [256, 128, 2048], P(('views', 'depth'), 'lat'), parts along dimension 0, may hold values from -6 to 6
- shift_table: int32 [256], P('views'), parts along dimension 0, may hold values from 0 to 48, as said below
- slab_order: int32 [16, 2], P(('views', 'lat')), parts along dimension 0, may hold values from 0 to 1, each once within a row
- centers: float32 [8], replicated, may hold values from -2 to 2
- widths: float32 [8], replicated, may hold values from 0.5 to 4
- extinct: float32 [8], replicated, may hold values from 0.2 to 3
- colors: float32 [3, 8], replicated, may hold values from 0 to 1
Outputs:
- image: float32 [4, 256, 2048], P(None, ('views', 'lat'), 'depth'), parts along dimension 1
The draws below stay inside these ranges and needn't reach their ends.
There are 2 independent parts, one for each index of `views`. The reference program is written for one: setup_inputs(seed, part) draws one part's arguments, and reference() takes and returns one part's arrays. A program takes and returns all parts, laid end to end along the dimension named above; an argument that names none is the same for every part. Nothing has to cross between parts.
Inputs may be any that keep to these rules, and one draw needn't show every extreme that they name: `shift_table`: every slice's shift lies in 0 to 48; some slice has shift 0 and some slice has shift exactly 48. `slab_order`: each row is a permutation of the slab indices; its entry 0 is the slab nearest the eye for that band of rows.
All inputs are finite; a program needn't handle non-finite values.
Results may differ from the reference program's by a relative error of at most 0.0003.
Values may be sent and summed in bfloat16 or wider, within the bound.
No kernel may reach another device: no remote copies, remote signals or barrier semaphores. Data moves between devices by JAX's collectives and lax.ppermute only.
A program may use at most 128 MiB of HBM per device.

```python
import math
import jax
import jax.numpy as jnp
from jax import lax

NX = 2048
ROWS_DEV = 16
LOBES = 8
NY = 128
NZ = 128
N_DEPTH = 2
N_LAT = 8


def draw_shift_table(key, part):
    values = jax.random.randint(key, (NZ,), 0, 3 * ROWS_DEV + 1, dtype=jnp.int32)
    where_high = jax.random.randint(jax.random.fold_in(key, 11), (), 0, NZ, dtype=jnp.int32)
    values = values.at[where_high].set(3 * ROWS_DEV)
    values = values.at[(where_high + 1) % NZ].set(0)
    return values


def block_levels(stream_key, dims, shards, low, top_value):
    gain = 1.0
    for position, parts in shards:
        steps = jax.random.uniform(jax.random.fold_in(jax.random.fold_in(stream_key, 6), position), (parts,), jnp.float32, low / len(shards), top_value / len(shards))
        gain = gain * jnp.repeat(jnp.exp(steps), dims[position] // parts).reshape((-1,) + (1,) * (len(dims) - 1 - position))
    return gain


def centred(stream_key, extent, width, bound, shards=(), kind=jnp.bfloat16):
    values = jax.random.normal(stream_key, extent, jnp.float32) * width
    if len(shards) > 0:
        values = block_levels(stream_key, extent, shards, -0.22, 0.18) * values
    return jnp.clip(values, min=-bound, max=bound).astype(kind)


def setup_inputs(seed: int = 0, part: int = 0) -> dict:
    key_of = jax.random.split(jax.random.key(seed), 8)
    part_splits = jax.random.split(jax.random.fold_in(key_of[7], part), 8)
    return {
        "volume": centred(part_splits[0], (NZ, NY, NX), 1.0, 6.0, ((0, 2), (1, 8))),
        "shift_table": draw_shift_table(jax.random.fold_in(jax.random.fold_in(key_of[7], part), 71), part),
        "slab_order": jax.vmap(lambda own: jax.random.permutation(own, N_DEPTH))(jax.random.split(part_splits[2], N_LAT)).reshape((N_LAT, N_DEPTH)).astype(jnp.int32),
        "centers": jnp.clip(jax.random.uniform(key_of[3], (LOBES,), jnp.float32, -2.0, 2.0), -2.0, 2.0),
        "widths": jnp.clip(jnp.exp(jax.random.uniform(key_of[4], (LOBES,), jnp.float32, math.log(0.5), math.log(4.0))), 0.5, 4.0),
        "extinct": jnp.clip(jnp.exp(jax.random.uniform(key_of[5], (LOBES,), jnp.float32, math.log(0.2), math.log(3.0))), 0.2, 3.0),
        "colors": jnp.clip(jax.random.uniform(key_of[6], (3, LOBES), jnp.float32, 0.0, 1.0), 0.0, 1.0),
    }


def classify(samples, centers, widths, extinct, colors, inv_depth):
    optical = jnp.zeros(samples.shape, jnp.float32)
    emission = jnp.zeros((3,) + samples.shape, jnp.float32)
    for lobe_index in range(centers.shape[0]):
        lobe_value = jnp.exp(-jnp.square(samples - centers[lobe_index]) * widths[lobe_index])
        optical = optical + extinct[lobe_index] * lobe_value
        emission = emission + colors[:, lobe_index].reshape((3,) + (1,) * samples.ndim) * lobe_value[None]
    return optical * inv_depth, emission


def composite(padded, shift_table, centers, widths, extinct, colors, forward, inv_depth):
    slice_count = padded.shape[0]
    row_count = padded.shape[1] - 3 * ROWS_DEV
    col_count = padded.shape[2]

    def advance(running, counter):
        depth_sum, color = running
        if forward:
            slice_index = counter
        else:
            slice_index = (slice_count - 1 - counter).astype(jnp.int32)
        offset = shift_table[slice_index].astype(jnp.int32)
        slice_plane = lax.dynamic_slice(padded, (slice_index, offset, jnp.int32(0)), (1, row_count, col_count))[0]
        optical, emission = classify(slice_plane.astype(jnp.float32), centers, widths, extinct, colors, inv_depth)
        weight = jnp.exp(-depth_sum) * (1.0 - jnp.exp(-optical))
        return (depth_sum + optical, color + weight[None] * emission), None

    start = (jnp.zeros((row_count, col_count), jnp.float32), jnp.zeros((3, row_count, col_count), jnp.float32))
    (depth_sum, color), _ = lax.scan(advance, start, jnp.arange(slice_count, dtype=jnp.int32))
    return depth_sum, color


def reference(volume, shift_table, slab_order, centers, widths, extinct, colors):
    reach = 3 * ROWS_DEV
    padded = jnp.pad(volume, ((0, 0), (0, reach), (0, 0)))
    inv_depth = 1.0 / NZ
    depth_sum, color_front = composite(padded, shift_table, centers, widths, extinct, colors, True, inv_depth)
    depth_back, color_back = composite(padded, shift_table, centers, widths, extinct, colors, False, inv_depth)
    row_forward = jnp.repeat(slab_order[:, 0] == 0, ROWS_DEV)
    color = jnp.where(row_forward[None, :, None], color_front, color_back)
    return jnp.concatenate([color, (1.0 - jnp.exp(-depth_sum))[None]], axis=0)
```

```python
import functools
import jax, jax.numpy as jnp
from jax import lax
from jax.experimental import pallas as pl
from jax.experimental.pallas import tpu as pltpu
from jax.sharding import PartitionSpec as P

LANES = 128
SUB = 8
LOG2E = 1.4426950408889634
LN2 = 0.6931471805599453
CHANNELS = 4


def compose_kernel(first, last, chunk_start, slices, rows, halo, inv_depth, unroll,
                   meta, shifts, sign_own, centers, widths, extinct, colors,
                   own, recv, below, above, *rest):
    if first:
        state_in, (out, scratch) = None, rest
    else:
        state_in, out, scratch = rest
    lobes = centers.shape[0]
    band = 2 * rows
    filled = halo + band + halo
    tail = scratch.shape[1] - filled
    parity, tile_lo, tile_hi = meta[0], meta[1], meta[2]
    shift_base = meta[3] + chunk_start
    at_own = pl.multiple_of(halo + parity * rows, SUB)
    at_recv = pl.multiple_of(halo + rows - parity * rows, SUB)

    def splat(v):
        return jnp.full((SUB, LANES), v, jnp.float32)

    gain = [splat(extinct[k]) * (LOG2E * inv_depth) for k in range(lobes)]
    slope = [jnp.sqrt(splat(widths[k]) * LOG2E) for k in range(lobes)]
    offset = [slope[k] * splat(centers[k]) for k in range(lobes)]
    level = [jnp.log(gain[k]) * LOG2E for k in range(lobes)]

    @pl.when(pl.program_id(0) == 0)
    def _():
        scratch[:, filled:, :] = jnp.zeros((scratch.shape[0], tail, LANES), jnp.float32)

    for cb in range(recv.shape[-1] // LANES):
        cols = slice(cb * LANES, (cb + 1) * LANES)

        def fill(s, carry):
            scratch[s, 0:halo, :] = below[s, :, cols].astype(jnp.float32)
            scratch[s, pl.ds(at_own, rows), :] = own[s, :, cols].astype(jnp.float32)
            scratch[s, pl.ds(at_recv, rows), :] = recv[s, :, cols].astype(jnp.float32)
            scratch[s, halo + band:filled, :] = above[s, :, cols].astype(jnp.float32)
            return carry

        lax.fori_loop(0, slices, fill, 0, unroll=2)
        if first:
            scratch[slices, 0:halo, :] = below[slices, :, cols].astype(jnp.float32)
            scratch[slices, pl.ds(at_own, rows), :] = jnp.full((rows, LANES), sign_own[0], jnp.float32)
            scratch[slices, pl.ds(at_recv, rows), :] = recv[slices, :, cols].astype(jnp.float32)

        def tile(t, carry):
            row = pl.multiple_of(t * SUB, SUB)
            here = pl.ds(row, SUB)
            if first:
                sign = scratch[slices, here, :]
                depth = jnp.zeros((SUB, LANES), jnp.float32)
                acc = [jnp.zeros((SUB, LANES), jnp.float32) for _ in range(lobes)]
            else:
                sign = state_in[lobes + 1, here, cols]
                depth = state_in[lobes, here, cols]
                acc = [state_in[k, here, cols] for k in range(lobes)]
            trans = jnp.exp2(depth * sign)

            def body(j, c):
                depth, trans, acc = c
                for u in range(unroll):
                    s = j * unroll + u
                    x = scratch[s, pl.ds(shifts[shift_base + s] + row, SUB), :]
                    lobe = []
                    optical = None
                    for k in range(lobes):
                        t_k = x * slope[k] - offset[k]
                        e = jnp.exp2(level[k] - t_k * t_k)
                        lobe.append(e)
                        optical = e if optical is None else optical + e
                    depth = depth + optical
                    new = jnp.exp2(depth * sign)
                    step = new - trans
                    acc = [acc[k] + step * lobe[k] for k in range(lobes)]
                    trans = new
                return depth, trans, acc

            depth, trans, acc = lax.fori_loop(0, slices // unroll, body, (depth, trans, acc))
            if last:
                norm = jnp.where(sign < 0, splat(-1.0), 1.0 / trans)
                for c in range(colors.shape[0]):
                    total = None
                    for k in range(lobes):
                        term = acc[k] * (splat(colors[c, k]) / gain[k])
                        total = term if total is None else total + term
                    out[c, here, cols] = total * norm
                out[CHANNELS - 1, here, cols] = depth * LN2
                out[CHANNELS, here, cols] = sign
            else:
                for k in range(lobes):
                    out[k, here, cols] = acc[k]
                out[lobes, here, cols] = depth
                out[lobes + 1, here, cols] = sign
            return carry

        lax.fori_loop(tile_lo, tile_hi, tile, 0)


def compose(meta, shifts, sign_own, params, volume, recv, below, above, state,
            *, first, last, part, chunk_start, slices, width, inv_depth, unroll):
    rows = volume.shape[1]
    halo = below.shape[1]
    band = 2 * rows
    cols = recv.shape[2]
    out_rows = band + halo
    lobes = params[0].shape[0]
    steps = cols // width
    half = steps // 2
    extra = 1 if first else 0
    cidx = chunk_start // slices
    smem = pl.BlockSpec(memory_space=pltpu.SMEM)

    def local_col(g, meta):
        if part is None:
            return g
        return (meta[4] if part else 1 - meta[4]) * half + g

    def own_map(g, meta, shifts):
        g = local_col(g, meta)
        return (cidx, 0, (g // half) * (2 * half) + meta[0] * half + g % half)

    def plain(g, meta, shifts):
        return (0, 0, local_col(g, meta))

    in_specs = [smem] * 5 + [
        pl.BlockSpec((slices, rows, width), own_map),
        pl.BlockSpec((slices + extra, rows, width), plain),
        pl.BlockSpec((slices + extra, halo, width), plain),
        pl.BlockSpec((slices, halo, width), plain),
    ]
    args = [sign_own, *params, volume, recv, below, above]
    aliases = {}
    if not first:
        in_specs.append(pl.BlockSpec((lobes + 2, out_rows, width), plain))
        args.append(state)
    if not first and not last:
        aliases = {2 + len(args) - 1: 0}
    n_out = CHANNELS + 1 if last else lobes + 2
    out_cols = cols if part is None else cols // 2
    samples = slices * out_rows * out_cols
    return pl.pallas_call(
        functools.partial(compose_kernel, first, last, chunk_start, slices, rows, halo, inv_depth, unroll),
        out_shape=jax.ShapeDtypeStruct((n_out, out_rows, out_cols), jnp.float32),
        grid_spec=pltpu.PrefetchScalarGridSpec(
            num_scalar_prefetch=2,
            grid=(steps if part is None else half,),
            in_specs=in_specs,
            out_specs=pl.BlockSpec((n_out, out_rows, width), lambda g, meta, shifts: (0, 0, g)),
            scratch_shapes=[pltpu.VMEM((slices + extra, halo + band + halo + halo, LANES), jnp.float32)],
        ),
        input_output_aliases=aliases,
        cost_estimate=pl.CostEstimate(flops=samples * 60, transcendentals=samples * 9, bytes_accessed=samples * 3),
        name="compose_first" if first else "compose_last" if last else "compose_mid",
    )(meta, shifts, *args)


def merge_kernel(rows, lead, meta, mine, got, here, side, up, cross, image):
    parity, slab = meta[0], meta[4]
    image[:, 0:lead, :] = jnp.zeros((CHANNELS, lead, image.shape[2]), jnp.float32)
    a_sum, b_sum = mine[CHANNELS - 1], got[CHANNELS - 1]
    first = jnp.where(slab == 0, -1.0, 1.0) * mine[CHANNELS] > 0
    through = jnp.exp(-jnp.where(first, a_sum, b_sum))
    for c in range(CHANNELS - 1):
        a, b = mine[c], got[c]
        image[c, lead:, :] = jnp.where(first, a, b) + through * jnp.where(first, b, a)
    image[CHANNELS - 1, lead:, :] = 1.0 - jnp.exp(-(a_sum + b_sum))
    band = 2 * rows

    def rows_at(start):
        return image[:, pl.ds(pl.multiple_of(start, SUB), rows), :]

    here[...] = rows_at(band + rows * parity)
    side[...] = rows_at(band + rows - rows * parity)
    up[...] = rows_at(rows * parity)
    cross[...] = rows_at(rows - rows * parity)


def merge(meta, mine, got, rows, lead):
    out_rows, cols = mine.shape[1:]
    width = 2 * LANES
    spec = pl.BlockSpec((CHANNELS, rows, width), lambda g, meta: (0, 0, g))
    shape = jax.ShapeDtypeStruct((CHANNELS, rows, cols), jnp.float32)
    return pl.pallas_call(
        functools.partial(merge_kernel, rows, lead),
        out_shape=[shape] * 4,
        grid_spec=pltpu.PrefetchScalarGridSpec(
            num_scalar_prefetch=1,
            grid=(cols // width,),
            in_specs=[
                pl.BlockSpec((CHANNELS + 1, out_rows, width), lambda g, meta: (0, 0, g)),
                pl.BlockSpec((CHANNELS, out_rows, width), lambda g, meta: (0, 0, g)),
            ],
            out_specs=[spec] * 4,
            scratch_shapes=[pltpu.VMEM((CHANNELS, lead + out_rows, width), jnp.float32)],
        ),
        name="merge",
    )(meta, mine, got)


CHUNKS = 4


def local(volume, shift_table, slab_order, centers, widths, extinct, colors):
    slab_count = lax.axis_size("depth")
    slab = lax.axis_index("depth")
    n = lax.axis_size("lat")
    me = lax.axis_index("lat")
    pair, parity = me // 2, me % 2
    slice_count, rows, col_count = volume.shape
    band = 2 * rows
    halo = 3 * rows // 2
    quarter = col_count // 4
    inv_depth = 1.0 / (slice_count * slab_count)
    chunk = slice_count // CHUNKS
    swap = [(i, i ^ 1) for i in range(n)]
    down = [(i, i - 2) for i in range(2, n)]
    up = [(i - 2, i) for i in range(2, n)]
    cross = [(i, (i ^ 1) - 2) for i in range(2, n)]
    is_last = pair == n // 2 - 1
    meta = jnp.stack([
        parity,
        jnp.where(pair == 0, halo // SUB, 0),
        jnp.where(is_last, (band + halo) // SUB, band // SUB),
        slab * slice_count,
        slab,
    ]).astype(jnp.int32)
    sign_own = jnp.where(slab_order[:, 0] == 0, -1.0, 1.0)
    params = (centers, widths, extinct, colors)

    def half(block, which):
        parts = [
            lax.dynamic_slice_in_dim(block, s * 2 * quarter + which * quarter, quarter, 2)
            for s in range(2)
        ]
        return jnp.concatenate(parts, axis=2)

    state = None
    for c in range(CHUNKS):
        block = volume[c * chunk:(c + 1) * chunk]
        give, own = half(block, 1 - parity), half(block, parity)
        if c == 0:
            flag = jnp.full((1, rows, 2 * quarter), sign_own[0], volume.dtype)
            give, own = jnp.concatenate([give, flag]), jnp.concatenate([own, flag])
        recv = lax.ppermute(give, "lat", swap)
        even = jnp.where(parity == 0, own, recv)
        odd = jnp.where(parity == 0, recv, own)
        upper = jnp.concatenate([even, odd[:, :halo - rows]], axis=1)[:chunk]
        lower = jnp.concatenate([even[:, band - halo:], odd], axis=1)
        above = lax.ppermute(upper, "lat", down)
        below = lax.ppermute(lower, "lat", up)
        run = functools.partial(
            compose, meta, shift_table, sign_own, params, volume, recv, below, above, state,
            first=c == 0, last=c == CHUNKS - 1, chunk_start=c * chunk, slices=chunk, width=2 * LANES,
            inv_depth=inv_depth, unroll=16)
        if c < CHUNKS - 1:
            state = run(part=None)
        else:
            give = run(part=0)
            mine = run(part=1)
    got = lax.ppermute(give[:CHANNELS], "depth", [(0, 1), (1, 0)])
    lead = band - halo
    from_pair, side, upper, diagonal = merge(meta, mine, got, rows, lead)
    from_side = lax.ppermute(side, "lat", swap)
    from_up = lax.ppermute(upper, "lat", down)
    from_cross = lax.ppermute(diagonal, "lat", cross)
    index = rows * parity + jnp.arange(rows)
    inside = (is_last | (index < lead))[None, :, None]
    a = jnp.where(inside, from_pair, from_up)
    b = jnp.where(inside, from_side, from_cross)
    return jnp.where(parity == 0, jnp.concatenate([a, b], axis=2), jnp.concatenate([b, a], axis=2))


def solution(mesh):
    in_specs = (
        P(("views", "depth"), "lat", None),
        P("views"),
        P(("views", "lat"), None),
        P(),
        P(),
        P(),
        P(),
    )
    out_specs = P(None, ("views", "lat"), "depth")

    return jax.shard_map(local, mesh=mesh, in_specs=in_specs, out_specs=out_specs, check_vma=False)
```

```python
import functools
import jax, jax.numpy as jnp
from jax import lax
from jax.experimental import pallas as pl
from jax.experimental.pallas import tpu as pltpu
from jax.sharding import PartitionSpec as P

LANES = 128
SUB = 8
LOG2E = 1.4426950408889634
LN2 = 0.6931471805599453
CHANNELS = 4
PARITY, TILE_LO, TILE_HI, SHIFT_BASE, SLAB = range(5)
SMEM = pl.BlockSpec(memory_space=pltpu.SMEM)
VMEM = pl.BlockSpec(memory_space=pltpu.VMEM)
PARAMS = pltpu.CompilerParams(vmem_limit_bytes=24 * 2**20)


def lanes_at(start):
    return pl.ds(pl.multiple_of(start, LANES), LANES)


def volume_lane(block, blocks, which):
    per = blocks // 2
    slab = block // per
    return ((2 * slab + which) * per + block - slab * per) * LANES


def compose_kernel(first, last, part, chunk_start, slices, rows, halo, inv_depth, unroll,
                   meta, shifts, sign_own, centers, widths, extinct, colors,
                   volume, recv, below, above, *rest):
    if first:
        state_in, (out, scratch) = None, rest
    else:
        state_in, out, scratch = rest
    lobes = centers.shape[0]
    band = 2 * rows
    filled = halo + band + halo
    tail = scratch.shape[1] - filled
    parity, tile_lo, tile_hi = meta[PARITY], meta[TILE_LO], meta[TILE_HI]
    shift_base = meta[SHIFT_BASE] + chunk_start
    at_own = pl.multiple_of(halo + parity * rows, SUB)
    at_recv = pl.multiple_of(halo + rows - parity * rows, SUB)
    blocks = recv.shape[-1] // LANES

    def splat(v):
        return jnp.full((SUB, LANES), v, jnp.float32)

    gain = [splat(extinct[k]) * (LOG2E * inv_depth) for k in range(lobes)]
    slope = [jnp.sqrt(splat(widths[k]) * LOG2E) for k in range(lobes)]
    offset = [slope[k] * splat(centers[k]) for k in range(lobes)]
    level = [jnp.log(gain[k]) * LOG2E for k in range(lobes)]

    scratch[:, filled:, :] = jnp.zeros((scratch.shape[0], tail, LANES), jnp.float32)

    def column(block, carry):
        if part is None:
            source, target = block, block
        else:
            keep = meta[SLAB] if part else 1 - meta[SLAB]
            source, target = keep * (blocks // 2) + block, block
        cols = lanes_at(source * LANES)
        here_cols = lanes_at(target * LANES)
        own_cols = lanes_at(volume_lane(source, blocks, parity))

        def fill(s, carry):
            scratch[s, 0:halo, :] = below[s, :, cols].astype(jnp.float32)
            scratch[s, pl.ds(at_own, rows), :] = volume[chunk_start + s, :, own_cols].astype(jnp.float32)
            scratch[s, pl.ds(at_recv, rows), :] = recv[s, :, cols].astype(jnp.float32)
            scratch[s, halo + band:filled, :] = above[s, :, cols].astype(jnp.float32)
            return carry

        lax.fori_loop(0, slices, fill, 0, unroll=4)
        if first:
            scratch[slices, 0:halo, :] = below[slices, :, cols].astype(jnp.float32)
            scratch[slices, pl.ds(at_own, rows), :] = jnp.full((rows, LANES), sign_own[0], jnp.float32)
            scratch[slices, pl.ds(at_recv, rows), :] = recv[slices, :, cols].astype(jnp.float32)

        def tile(t, carry):
            row = pl.multiple_of(t * SUB, SUB)
            here = pl.ds(row, SUB)
            if first:
                sign = scratch[slices, here, :]
                depth = jnp.zeros((SUB, LANES), jnp.float32)
                acc = [jnp.zeros((SUB, LANES), jnp.float32) for _ in range(lobes)]
            else:
                sign = state_in[lobes + 1, here, cols]
                depth = state_in[lobes, here, cols]
                acc = [state_in[k, here, cols] for k in range(lobes)]
            trans = jnp.exp2(depth * sign)

            def body(j, c):
                depth, trans, acc = c
                for u in range(unroll):
                    s = j * unroll + u
                    x = scratch[s, pl.ds(shifts[shift_base + s] + row, SUB), :]
                    lobe = []
                    optical = None
                    for k in range(lobes):
                        t_k = x * slope[k] - offset[k]
                        e = jnp.exp2(level[k] - t_k * t_k)
                        lobe.append(e)
                        optical = e if optical is None else optical + e
                    depth = depth + optical
                    new = jnp.exp2(depth * sign)
                    step = new - trans
                    acc = [acc[k] + step * lobe[k] for k in range(lobes)]
                    trans = new
                return depth, trans, acc

            depth, trans, acc = lax.fori_loop(0, slices // unroll, body, (depth, trans, acc))
            if last:
                norm = jnp.where(sign < 0, splat(-1.0), 1.0 / trans)
                for c in range(colors.shape[0]):
                    total = None
                    for k in range(lobes):
                        term = acc[k] * (splat(colors[c, k]) / gain[k])
                        total = term if total is None else total + term
                    out[c, here, here_cols] = total * norm
                out[CHANNELS - 1, here, here_cols] = depth * LN2
                out[CHANNELS, here, here_cols] = sign
            else:
                for k in range(lobes):
                    out[k, here, here_cols] = acc[k]
                out[lobes, here, here_cols] = depth
                out[lobes + 1, here, here_cols] = sign
            return carry

        lax.fori_loop(tile_lo, tile_hi, tile, 0)
        return carry

    lax.fori_loop(0, blocks if part is None else blocks // 2, column, 0)


def compose(meta, shifts, sign_own, params, volume, recv, below, above, state,
            *, first, last, part, chunk_start, slices, inv_depth, unroll):
    rows = volume.shape[1]
    halo = below.shape[1]
    band = 2 * rows
    cols = recv.shape[2]
    out_rows = band + halo
    lobes = params[0].shape[0]
    args = [meta, shifts, sign_own, *params, volume, recv, below, above]
    specs = [SMEM] * 7 + [VMEM] * 4
    aliases = {}
    if not first:
        args.append(state)
        specs.append(VMEM)
        if not last:
            aliases = {len(args) - 1: 0}
    n_out = CHANNELS + 1 if last else lobes + 2
    out_cols = cols if part is None else cols // 2
    samples = slices * out_rows * out_cols
    return pl.pallas_call(
        functools.partial(compose_kernel, first, last, part, chunk_start, slices, rows, halo, inv_depth, unroll),
        out_shape=jax.ShapeDtypeStruct((n_out, out_rows, out_cols), jnp.float32),
        in_specs=specs,
        out_specs=VMEM,
        scratch_shapes=[pltpu.VMEM((slices + (1 if first else 0), filled_rows(rows, halo), LANES), jnp.float32)],
        input_output_aliases=aliases,
        compiler_params=PARAMS,
        cost_estimate=pl.CostEstimate(flops=samples * 60, transcendentals=samples * 9, bytes_accessed=samples * 3),
        name="compose_first" if first else "compose_last" if last else "compose_mid",
    )(*args)


def filled_rows(rows, halo):
    return 2 * rows + 3 * halo


def split_kernel(slices, chunk_start, meta, sign_own, volume, out):
    blocks = out.shape[2] // LANES
    other = 1 - meta[PARITY]
    for b in range(blocks):
        source = lanes_at(volume_lane(b, blocks, other))
        out[0:slices, :, b * LANES:(b + 1) * LANES] = volume[chunk_start:chunk_start + slices, :, source]
    if out.shape[0] > slices:
        sign = jnp.full((out.shape[1], out.shape[2]), sign_own[0], jnp.float32)
        out[slices] = sign.astype(out.dtype)


def split(meta, sign_own, volume, chunk_start, slices, first):
    rows, cols = volume.shape[1], volume.shape[2]
    total = slices + (1 if first else 0)
    return pl.pallas_call(
        functools.partial(split_kernel, slices, chunk_start),
        out_shape=jax.ShapeDtypeStruct((total, rows, cols // 2), volume.dtype),
        in_specs=[SMEM, SMEM, VMEM],
        out_specs=VMEM,
        compiler_params=PARAMS,
        cost_estimate=pl.CostEstimate(flops=0, transcendentals=0, bytes_accessed=2 * total * rows * cols),
        name="split",
    )(meta, sign_own, volume)


def pack_kernel(slices, chunk_start, rows, halo, meta, sign_own, volume, recv, upper, lower):
    blocks = recv.shape[2] // LANES
    odd_in_upper = halo - rows
    even_from = 2 * rows - halo
    flags = recv.shape[0] > slices
    parity = meta[PARITY]

    def place(own_is_even):
        for b in range(blocks):
            cols = slice(b * LANES, (b + 1) * LANES)
            source = lanes_at(volume_lane(b, blocks, parity))

            def one(s, carry):
                own = volume[chunk_start + s, :, source]
                other = recv[s, :, cols]
                even, odd = (own, other) if own_is_even else (other, own)
                upper[s, 0:rows, cols] = even
                upper[s, rows:halo, cols] = odd[0:odd_in_upper]
                lower[s, 0:halo - rows, cols] = even[even_from:rows]
                lower[s, halo - rows:halo, cols] = odd
                return carry

            lax.fori_loop(0, slices, one, 0, unroll=4)
        if flags:
            own = jnp.full((rows, lower.shape[2]), sign_own[0], jnp.float32).astype(lower.dtype)
            other = recv[slices]
            even, odd = (own, other) if own_is_even else (other, own)
            lower[slices, 0:halo - rows, :] = even[even_from:rows]
            lower[slices, halo - rows:halo, :] = odd

    @pl.when(parity == 0)
    def _():
        place(True)

    @pl.when(parity == 1)
    def _():
        place(False)


def pack(meta, sign_own, volume, recv, chunk_start, slices, halo):
    rows = volume.shape[1]
    total, _, cols = recv.shape
    return pl.pallas_call(
        functools.partial(pack_kernel, slices, chunk_start, rows, halo),
        out_shape=[
            jax.ShapeDtypeStruct((slices, halo, cols), recv.dtype),
            jax.ShapeDtypeStruct((total, halo, cols), recv.dtype),
        ],
        in_specs=[SMEM, SMEM, VMEM, VMEM],
        out_specs=[VMEM, VMEM],
        compiler_params=PARAMS,
        cost_estimate=pl.CostEstimate(flops=0, transcendentals=0, bytes_accessed=4 * total * rows * cols),
        name="pack",
    )(meta, sign_own, volume, recv)


def merge_kernel(rows, lead, meta, mine, got, here, side, up, cross, image):
    parity, slab = meta[PARITY], meta[SLAB]
    band = 2 * rows
    blocks = mine.shape[2] // LANES
    image[:, 0:lead, :] = jnp.zeros((CHANNELS, lead, LANES), jnp.float32)
    for b in range(blocks):
        cols = slice(b * LANES, (b + 1) * LANES)
        a_sum, b_sum = mine[CHANNELS - 1, :, cols], got[CHANNELS - 1, :, cols]
        first = jnp.where(slab == 0, -1.0, 1.0) * mine[CHANNELS, :, cols] > 0
        through = jnp.exp(-jnp.where(first, a_sum, b_sum))
        for c in range(CHANNELS - 1):
            a, g = mine[c, :, cols], got[c, :, cols]
            image[c, lead:, :] = jnp.where(first, a, g) + through * jnp.where(first, g, a)
        image[CHANNELS - 1, lead:, :] = 1.0 - jnp.exp(-(a_sum + b_sum))

        def rows_at(start):
            return image[:, pl.ds(pl.multiple_of(start, SUB), rows), :]

        here[:, :, cols] = rows_at(band + rows * parity)
        side[:, :, cols] = rows_at(band + rows - rows * parity)
        up[:, :, cols] = rows_at(rows * parity)
        cross[:, :, cols] = rows_at(rows - rows * parity)


def merge(meta, mine, got, rows, lead):
    out_rows, cols = mine.shape[1:]
    shape = jax.ShapeDtypeStruct((CHANNELS, rows, cols), jnp.float32)
    return pl.pallas_call(
        functools.partial(merge_kernel, rows, lead),
        out_shape=[shape] * 4,
        in_specs=[SMEM, VMEM, VMEM],
        out_specs=[VMEM] * 4,
        scratch_shapes=[pltpu.VMEM((CHANNELS, lead + out_rows, LANES), jnp.float32)],
        compiler_params=PARAMS,
        name="merge",
    )(meta, mine, got)


CHUNKS = (1, 2, 2, 2, 1)


def unroll_of(chunk):
    return max(u for u in range(1, 17) if chunk % u == 0)


def local(volume, shift_table, slab_order, centers, widths, extinct, colors):
    slab_count = lax.axis_size("depth")
    slab = lax.axis_index("depth")
    n = lax.axis_size("lat")
    me = lax.axis_index("lat")
    pair, parity = me // 2, me % 2
    slice_count, rows, _ = volume.shape
    band = 2 * rows
    halo = 3 * rows // 2
    inv_depth = 1.0 / (slice_count * slab_count)
    swap = [(i, i ^ 1) for i in range(n)]
    down = [(i, i - 2) for i in range(2, n)]
    up = [(i - 2, i) for i in range(2, n)]
    cross = [(i, (i ^ 1) - 2) for i in range(2, n)]
    is_last = pair == n // 2 - 1
    meta = jnp.stack([
        parity,
        jnp.where(pair == 0, halo // SUB, 0),
        jnp.where(is_last, (band + halo) // SUB, band // SUB),
        slab * slice_count,
        slab,
    ]).astype(jnp.int32)
    sign_own = jnp.where(slab_order[:, 0] == 0, -1.0, 1.0)
    params = (centers, widths, extinct, colors)

    state = None
    start = 0
    for c, part in enumerate(CHUNKS):
        chunk = slice_count * part // sum(CHUNKS)
        first, last = c == 0, c == len(CHUNKS) - 1
        give = split(meta, sign_own, volume, start, chunk, first)
        recv = lax.ppermute(give, "lat", swap)
        upper, lower = pack(meta, sign_own, volume, recv, start, chunk, halo)
        above = lax.ppermute(upper, "lat", down)
        below = lax.ppermute(lower, "lat", up)
        run = functools.partial(
            compose, meta, shift_table, sign_own, params, volume, recv, below, above, state,
            first=first, last=last, chunk_start=start, slices=chunk,
            inv_depth=inv_depth, unroll=unroll_of(chunk))
        if last:
            give = run(part=0)
            mine = run(part=1)
        else:
            state = run(part=None)
        start += chunk
    got = lax.ppermute(give, "depth", [(0, 1), (1, 0)])
    lead = band - halo
    from_pair, side, upper, diagonal = merge(meta, mine, got, rows, lead)
    from_side = lax.ppermute(side, "lat", swap)
    from_up = lax.ppermute(upper, "lat", down)
    from_cross = lax.ppermute(diagonal, "lat", cross)
    index = rows * parity + jnp.arange(rows)
    inside = (is_last | (index < lead))[None, :, None]
    a = jnp.where(inside, from_pair, from_up)
    b = jnp.where(inside, from_side, from_cross)
    return jnp.where(parity == 0, jnp.concatenate([a, b], axis=2), jnp.concatenate([b, a], axis=2))


def solution(mesh):
    in_specs = (
        P(("views", "depth"), "lat", None),
        P("views"),
        P(("views", "lat"), None),
        P(),
        P(),
        P(),
        P(),
    )
    out_specs = P(None, ("views", "lat"), "depth")

    return jax.shard_map(local, mesh=mesh, in_specs=in_specs, out_specs=out_specs, check_vma=False)
```

```python
import functools
import math
import jax, jax.numpy as jnp
from jax import lax
from jax.experimental import pallas as pl
from jax.experimental.pallas import tpu as pltpu
from jax.sharding import PartitionSpec as P

LANES = 128
SUB = 8
LOG2E = 1.4426950408889634
LN2 = 0.6931471805599453
CHANNELS = 4
PARITY, TILE_LO, TILE_HI, SHIFT_BASE, SLAB = range(5)
SMEM = pl.BlockSpec(memory_space=pltpu.SMEM)
VMEM = pl.BlockSpec(memory_space=pltpu.VMEM)
PARAMS = pltpu.CompilerParams(vmem_limit_bytes=24 * 2**20)


def lanes_at(start):
    return pl.ds(pl.multiple_of(start, LANES), LANES)


def volume_lane(block, blocks, which):
    per = blocks // 2
    slab = block // per
    return ((2 * slab + which) * per + block - slab * per) * LANES


def lift_blocks(shift, halo):
    return jnp.maximum(halo - shift + SUB - 1, 0) // SUB


def sink_blocks(shift, halo):
    return jnp.maximum(shift - halo + SUB - 1, 0) // SUB


def slot(start, j, room):
    return jnp.minimum(start + j, room)


def room_for(slices, halo):
    usual = slices + 4 * math.sqrt(slices)
    return min(slices * (halo // SUB), int(usual))


def fits_kernel(chunks, halo, shifts, out):
    shift = shifts[...]
    total = shift.shape[1]
    index = lax.broadcasted_iota(jnp.int32, shift.shape, 1)
    lift = jnp.maximum(halo - shift + SUB - 1, 0) // SUB
    sink = jnp.maximum(shift - halo + SUB - 1, 0) // SUB
    excess = jnp.zeros((1, 1), jnp.int32)
    start = 0
    while start < total:
        for chunk in chunks:
            inside = (index >= start) & (index < start + chunk)
            room = room_for(chunk, halo)
            for need in (lift, sink):
                count = jnp.sum(jnp.where(inside, need, 0).astype(jnp.float32), axis=1, keepdims=True)
                excess = jnp.maximum(excess, count.astype(jnp.int32) - room)
            start += chunk
    out[...] = excess


def fits(shifts, chunks, halo):
    excess = pl.pallas_call(
        functools.partial(fits_kernel, chunks, halo),
        out_shape=jax.ShapeDtypeStruct((1, 1), jnp.int32),
        in_specs=[VMEM],
        out_specs=VMEM,
        name="fits",
    )(shifts.reshape(1, -1))
    return excess[0, 0] <= 0


def compose_kernel(first, last, part, packed, chunk_start, slices, rows, halo, inv_depth, unroll,
                   meta, shifts, sign_own, centers, widths, extinct, colors,
                   volume, recv, below, above, *rest):
    if first:
        state_in, (out, scratch) = None, rest
    else:
        state_in, out, scratch = rest
    lobes = centers.shape[0]
    band = 2 * rows
    room = above.shape[0] - 1
    filled = halo + band + halo
    tail = scratch.shape[2] - filled
    parity, tile_lo, tile_hi = meta[PARITY], meta[TILE_LO], meta[TILE_HI]
    shift_base = meta[SHIFT_BASE] + chunk_start
    at_own = pl.multiple_of(halo + parity * rows, SUB)
    at_recv = pl.multiple_of(halo + rows - parity * rows, SUB)
    blocks = recv.shape[-1] // LANES

    def splat(v):
        return jnp.full((SUB, LANES), v, jnp.float32)

    gain = [splat(extinct[k]) * (LOG2E * inv_depth) for k in range(lobes)]
    slope = [jnp.sqrt(splat(widths[k]) * LOG2E) for k in range(lobes)]
    offset = [slope[k] * splat(centers[k]) for k in range(lobes)]
    level = [jnp.log(gain[k]) * LOG2E for k in range(lobes)]

    count = scratch.shape[0]
    if part is None:
        base = jnp.int32(0)
    else:
        base = (meta[SLAB] if part else 1 - meta[SLAB]) * count
    cols_of = [lanes_at((base + b) * LANES) for b in range(count)]
    own_of = [lanes_at(volume_lane(base + b, blocks, parity)) for b in range(count)]

    def fill(s, carry):
        lift, sink = carry
        shift = shifts[shift_base + s]
        for j in range(halo // SUB):
            low, high = slot(lift, j, room), slot(sink, j, room)
            to_low, to_high = halo - (j + 1) * SUB, halo + band + j * SUB
            for b in range(count):
                if packed:
                    scratch[b, s, to_low:to_low + SUB, :] = below[low, :, cols_of[b]].astype(jnp.float32)
                    scratch[b, s, to_high:to_high + SUB, :] = above[high, :, cols_of[b]].astype(jnp.float32)
        for b in range(count):
            scratch[b, s, filled:, :] = jnp.zeros((tail, LANES), jnp.float32)
            scratch[b, s, pl.ds(at_own, rows), :] = volume[chunk_start + s, :, own_of[b]].astype(jnp.float32)
            scratch[b, s, pl.ds(at_recv, rows), :] = recv[s, :, cols_of[b]].astype(jnp.float32)
            if not packed:
                scratch[b, s, 0:halo, :] = below[s, :, cols_of[b]].astype(jnp.float32)
                scratch[b, s, halo + band:filled, :] = above[s, :, cols_of[b]].astype(jnp.float32)
        return lift + lift_blocks(shift, halo), sink + sink_blocks(shift, halo)

    lax.fori_loop(0, slices, fill, (jnp.int32(0), jnp.int32(0)))
    if first:
        for b in range(count):
            if packed:
                for j in range(halo // SUB):
                    to = halo - (j + 1) * SUB
                    scratch[b, slices, to:to + SUB, :] = below[room + 1 + j, :, cols_of[b]].astype(jnp.float32)
            else:
                scratch[b, slices, 0:halo, :] = below[slices, :, cols_of[b]].astype(jnp.float32)
            scratch[b, slices, pl.ds(at_own, rows), :] = jnp.full((rows, LANES), sign_own[0], jnp.float32)
            scratch[b, slices, pl.ds(at_recv, rows), :] = recv[slices, :, cols_of[b]].astype(jnp.float32)

    def column(block, carry):
        cols = lanes_at((base + block) * LANES)
        here_cols = lanes_at(block * LANES)

        def tile(t, carry):
            row = pl.multiple_of(t * SUB, SUB)
            here = pl.ds(row, SUB)
            if first:
                sign = scratch[block, slices, here, :]
                depth = jnp.zeros((SUB, LANES), jnp.float32)
                acc = [jnp.zeros((SUB, LANES), jnp.float32) for _ in range(lobes)]
            else:
                sign = state_in[lobes + 1, here, cols]
                depth = state_in[lobes, here, cols]
                acc = [state_in[k, here, cols] for k in range(lobes)]
            trans = jnp.exp2(depth * sign)

            def body(j, c):
                depth, trans, acc = c
                for u in range(unroll):
                    s = j * unroll + u
                    x = scratch[block, s, pl.ds(shifts[shift_base + s] + row, SUB), :]
                    lobe = []
                    optical = None
                    for k in range(lobes):
                        t_k = x * slope[k] - offset[k]
                        e = jnp.exp2(level[k] - t_k * t_k)
                        lobe.append(e)
                        optical = e if optical is None else optical + e
                    depth = depth + optical
                    new = jnp.exp2(depth * sign)
                    step = new - trans
                    acc = [acc[k] + step * lobe[k] for k in range(lobes)]
                    trans = new
                return depth, trans, acc

            depth, trans, acc = lax.fori_loop(0, slices // unroll, body, (depth, trans, acc))
            if last:
                norm = jnp.where(sign < 0, splat(-1.0), 1.0 / trans)
                for c in range(colors.shape[0]):
                    total = None
                    for k in range(lobes):
                        term = acc[k] * (splat(colors[c, k]) / gain[k])
                        total = term if total is None else total + term
                    out[c, here, here_cols] = total * norm
                out[CHANNELS - 1, here, here_cols] = depth * LN2
                out[CHANNELS, here, here_cols] = sign
            else:
                for k in range(lobes):
                    out[k, here, here_cols] = acc[k]
                out[lobes, here, here_cols] = depth
                out[lobes + 1, here, here_cols] = sign
            return carry

        lax.fori_loop(tile_lo, tile_hi, tile, 0)
        return carry

    lax.fori_loop(0, count, column, 0)


def compose(meta, shifts, sign_own, params, volume, recv, below, above, state,
            *, first, last, part, packed, chunk_start, slices, inv_depth, unroll):
    rows = volume.shape[1]
    halo = 3 * rows // 2
    band = 2 * rows
    cols = recv.shape[2]
    out_rows = band + halo
    lobes = params[0].shape[0]
    args = [meta, shifts, sign_own, *params, volume, recv, below, above]
    specs = [SMEM] * 7 + [VMEM] * 4
    aliases = {}
    if not first:
        args.append(state)
        specs.append(VMEM)
        if not last:
            aliases = {len(args) - 1: 0}
    n_out = CHANNELS + 1 if last else lobes + 2
    out_cols = cols if part is None else cols // 2
    samples = slices * out_rows * out_cols
    return pl.pallas_call(
        functools.partial(compose_kernel, first, last, part, packed, chunk_start, slices, rows, halo, inv_depth, unroll),
        out_shape=jax.ShapeDtypeStruct((n_out, out_rows, out_cols), jnp.float32),
        in_specs=specs,
        out_specs=VMEM,
        scratch_shapes=[pltpu.VMEM(
            (out_cols // LANES, slices + (1 if first else 0), filled_rows(rows, halo), LANES), jnp.float32)],
        input_output_aliases=aliases,
        compiler_params=PARAMS,
        cost_estimate=pl.CostEstimate(flops=samples * 60, transcendentals=samples * 9, bytes_accessed=samples * 3),
        name="compose_first" if first else "compose_last" if last else "compose_mid",
    )(*args)


def filled_rows(rows, halo):
    return 2 * rows + 3 * halo


def split_kernel(slices, chunk_start, meta, sign_own, volume, out):
    blocks = out.shape[2] // LANES
    other = 1 - meta[PARITY]
    for b in range(blocks):
        source = lanes_at(volume_lane(b, blocks, other))
        out[0:slices, :, b * LANES:(b + 1) * LANES] = volume[chunk_start:chunk_start + slices, :, source]
    if out.shape[0] > slices:
        sign = jnp.full((out.shape[1], out.shape[2]), sign_own[0], jnp.float32)
        out[slices] = sign.astype(out.dtype)


def split(meta, sign_own, volume, chunk_start, slices, first):
    rows, cols = volume.shape[1], volume.shape[2]
    total = slices + (1 if first else 0)
    return pl.pallas_call(
        functools.partial(split_kernel, slices, chunk_start),
        out_shape=jax.ShapeDtypeStruct((total, rows, cols // 2), volume.dtype),
        in_specs=[SMEM, SMEM, VMEM],
        out_specs=VMEM,
        compiler_params=PARAMS,
        cost_estimate=pl.CostEstimate(flops=0, transcendentals=0, bytes_accessed=2 * total * rows * cols),
        name="split",
    )(meta, sign_own, volume)


def pack_kernel(slices, chunk_start, rows, halo, meta, sign_own, volume, recv, upper, lower):
    blocks = recv.shape[2] // LANES
    odd_in_upper = halo - rows
    even_from = 2 * rows - halo
    flags = recv.shape[0] > slices
    parity = meta[PARITY]

    def place(own_is_even):
        for b in range(blocks):
            cols = slice(b * LANES, (b + 1) * LANES)
            source = lanes_at(volume_lane(b, blocks, parity))

            def one(s, carry):
                own = volume[chunk_start + s, :, source]
                other = recv[s, :, cols]
                even, odd = (own, other) if own_is_even else (other, own)
                upper[s, 0:rows, cols] = even
                upper[s, rows:halo, cols] = odd[0:odd_in_upper]
                lower[s, 0:halo - rows, cols] = even[even_from:rows]
                lower[s, halo - rows:halo, cols] = odd
                return carry

            lax.fori_loop(0, slices, one, 0, unroll=4)
        if flags:
            own = jnp.full((rows, lower.shape[2]), sign_own[0], jnp.float32).astype(lower.dtype)
            other = recv[slices]
            even, odd = (own, other) if own_is_even else (other, own)
            lower[slices, 0:halo - rows, :] = even[even_from:rows]
            lower[slices, halo - rows:halo, :] = odd

    @pl.when(parity == 0)
    def _():
        place(True)

    @pl.when(parity == 1)
    def _():
        place(False)


def pack(meta, sign_own, volume, recv, chunk_start, slices, halo):
    rows = volume.shape[1]
    total, _, cols = recv.shape
    return pl.pallas_call(
        functools.partial(pack_kernel, slices, chunk_start, rows, halo),
        out_shape=[
            jax.ShapeDtypeStruct((slices, halo, cols), recv.dtype),
            jax.ShapeDtypeStruct((total, halo, cols), recv.dtype),
        ],
        in_specs=[SMEM, SMEM, VMEM, VMEM],
        out_specs=[VMEM, VMEM],
        compiler_params=PARAMS,
        cost_estimate=pl.CostEstimate(flops=0, transcendentals=0, bytes_accessed=4 * total * rows * cols),
        name="pack",
    )(meta, sign_own, volume, recv)


def pack_blocks_kernel(slices, chunk_start, rows, halo, flags, meta, shifts, sign_own, volume, recv, upper, lower):
    blocks = recv.shape[2] // LANES
    parity = meta[PARITY]
    shift_base = meta[SHIFT_BASE] + chunk_start
    room = upper.shape[0] - 1

    def place(own_is_even):
        def one(s, carry):
            lift, sink = carry
            shift = shifts[shift_base + s]
            for b in range(blocks):
                cols = slice(b * LANES, (b + 1) * LANES)
                own = volume[chunk_start + s, :, lanes_at(volume_lane(b, blocks, parity))]
                other = recv[s, :, cols]
                even, odd = (own, other) if own_is_even else (other, own)
                pieces = [x[r:r + SUB] for x in (even, odd) for r in range(0, rows, SUB)]
                for j in range(halo // SUB):
                    upper[slot(sink, j, room), :, cols] = pieces[j]
                    lower[slot(lift, j, room), :, cols] = pieces[-1 - j]
            return lift + lift_blocks(shift, halo), sink + sink_blocks(shift, halo)

        lax.fori_loop(0, slices, one, (jnp.int32(0), jnp.int32(0)), unroll=2)
        if flags:
            own = jnp.full((rows, lower.shape[2]), sign_own[0], jnp.float32).astype(lower.dtype)
            other = recv[slices]
            even, odd = (own, other) if own_is_even else (other, own)
            pieces = [x[r:r + SUB] for x in (even, odd) for r in range(0, rows, SUB)]
            for j in range(halo // SUB):
                lower[room + 1 + j] = pieces[-1 - j]

    @pl.when(parity == 0)
    def _():
        place(True)

    @pl.when(parity == 1)
    def _():
        place(False)


def pack_blocks(meta, shifts, sign_own, volume, recv, chunk_start, slices, halo):
    rows = volume.shape[1]
    total, _, cols = recv.shape
    flags = total > slices
    slots = room_for(slices, halo) + 1
    return pl.pallas_call(
        functools.partial(pack_blocks_kernel, slices, chunk_start, rows, halo, flags),
        out_shape=[
            jax.ShapeDtypeStruct((slots, SUB, cols), recv.dtype),
            jax.ShapeDtypeStruct((slots + (halo // SUB if flags else 0), SUB, cols), recv.dtype),
        ],
        in_specs=[SMEM, SMEM, SMEM, VMEM, VMEM],
        out_specs=[VMEM, VMEM],
        compiler_params=PARAMS,
        cost_estimate=pl.CostEstimate(flops=0, transcendentals=0, bytes_accessed=4 * total * rows * cols),
        name="pack_blocks",
    )(meta, shifts, sign_own, volume, recv)


def merge_kernel(rows, lead, meta, mine, got, here, side, up, cross, image):
    parity, slab = meta[PARITY], meta[SLAB]
    band = 2 * rows
    blocks = mine.shape[2] // LANES
    image[:, 0:lead, :] = jnp.zeros((CHANNELS, lead, LANES), jnp.float32)
    for b in range(blocks):
        cols = slice(b * LANES, (b + 1) * LANES)
        a_sum, b_sum = mine[CHANNELS - 1, :, cols], got[CHANNELS - 1, :, cols]
        first = jnp.where(slab == 0, -1.0, 1.0) * mine[CHANNELS, :, cols] > 0
        through = jnp.exp(-jnp.where(first, a_sum, b_sum))
        for c in range(CHANNELS - 1):
            a, g = mine[c, :, cols], got[c, :, cols]
            image[c, lead:, :] = jnp.where(first, a, g) + through * jnp.where(first, g, a)
        image[CHANNELS - 1, lead:, :] = 1.0 - jnp.exp(-(a_sum + b_sum))

        def rows_at(start):
            return image[:, pl.ds(pl.multiple_of(start, SUB), rows), :]

        here[:, :, cols] = rows_at(band + rows * parity)
        side[:, :, cols] = rows_at(band + rows - rows * parity)
        up[:, :, cols] = rows_at(rows * parity)
        cross[:, :, cols] = rows_at(rows - rows * parity)


def merge(meta, mine, got, rows, lead):
    out_rows, cols = mine.shape[1:]
    shape = jax.ShapeDtypeStruct((CHANNELS, rows, cols), jnp.float32)
    return pl.pallas_call(
        functools.partial(merge_kernel, rows, lead),
        out_shape=[shape] * 4,
        in_specs=[SMEM, VMEM, VMEM],
        out_specs=[VMEM] * 4,
        scratch_shapes=[pltpu.VMEM((CHANNELS, lead + out_rows, LANES), jnp.float32)],
        compiler_params=PARAMS,
        name="merge",
    )(meta, mine, got)


CHUNKS = (2, 4, 5, 5)


def chunk_sizes(slice_count):
    return [slice_count * part // sum(CHUNKS) for part in CHUNKS]


def unroll_of(chunk):
    return max(u for u in range(1, 17) if chunk % u == 0)


def render(packed, volume, shift_table, slab_order, centers, widths, extinct, colors):
    slab_count = lax.axis_size("depth")
    slab = lax.axis_index("depth")
    n = lax.axis_size("lat")
    me = lax.axis_index("lat")
    pair, parity = me // 2, me % 2
    slice_count, rows, _ = volume.shape
    band = 2 * rows
    halo = 3 * rows // 2
    inv_depth = 1.0 / (slice_count * slab_count)
    swap = [(i, i ^ 1) for i in range(n)]
    down = [(i, i - 2) for i in range(2, n)]
    up = [(i - 2, i) for i in range(2, n)]
    cross = [(i, (i ^ 1) - 2) for i in range(2, n)]
    is_last = pair == n // 2 - 1
    meta = jnp.stack([
        parity,
        jnp.where(pair == 0, halo // SUB, 0),
        jnp.where(is_last, (band + halo) // SUB, band // SUB),
        slab * slice_count,
        slab,
    ]).astype(jnp.int32)
    sign_own = jnp.where(slab_order[:, 0] == 0, -1.0, 1.0)
    params = (centers, widths, extinct, colors)

    state = None
    start = 0
    for c, chunk in enumerate(chunk_sizes(slice_count)):
        first, last = c == 0, c == len(CHUNKS) - 1
        give = split(meta, sign_own, volume, start, chunk, first)
        recv = lax.ppermute(give, "lat", swap)
        if packed:
            upper, lower = pack_blocks(meta, shift_table, sign_own, volume, recv, start, chunk, halo)
        else:
            upper, lower = pack(meta, sign_own, volume, recv, start, chunk, halo)
        above = lax.ppermute(upper, "lat", down)
        below = lax.ppermute(lower, "lat", up)
        run = functools.partial(
            compose, meta, shift_table, sign_own, params, volume, recv, below, above, state,
            first=first, last=last, packed=packed, chunk_start=start, slices=chunk,
            inv_depth=inv_depth, unroll=unroll_of(chunk))
        if last:
            give = run(part=0)
            mine = run(part=1)
        else:
            state = run(part=None)
        start += chunk
    got = lax.ppermute(give, "depth", [(0, 1), (1, 0)])
    lead = band - halo
    from_pair, side, upper, diagonal = merge(meta, mine, got, rows, lead)
    from_side = lax.ppermute(side, "lat", swap)
    from_up = lax.ppermute(upper, "lat", down)
    from_cross = lax.ppermute(diagonal, "lat", cross)
    index = rows * parity + jnp.arange(rows)
    inside = (is_last | (index < lead))[None, :, None]
    a = jnp.where(inside, from_pair, from_up)
    b = jnp.where(inside, from_side, from_cross)
    return jnp.where(parity == 0, jnp.concatenate([a, b], axis=2), jnp.concatenate([b, a], axis=2))


def local(volume, shift_table, *rest):
    halo = 3 * volume.shape[1] // 2
    usual = fits(shift_table, chunk_sizes(volume.shape[0]), halo)

    def branch(packed):
        def run(*args):
            return render(packed, *args)

        return run

    return lax.cond(usual, branch(True), branch(False), volume, shift_table, *rest)


def solution(mesh):
    in_specs = (
        P(("views", "depth"), "lat", None),
        P("views"),
        P(("views", "lat"), None),
        P(),
        P(),
        P(),
        P(),
    )
    out_specs = P(None, ("views", "lat"), "depth")
    return jax.shard_map(local, mesh=mesh, in_specs=in_specs, out_specs=out_specs, check_vma=False)
```

```python
import functools
import math
import jax, jax.numpy as jnp
from jax import lax
from jax.experimental import pallas as pl
from jax.experimental.pallas import tpu as pltpu
from jax.sharding import PartitionSpec as P

LANES = 128
SUB = 8
LOG2E = 1.4426950408889634
LN2 = 0.6931471805599453
CHANNELS = 4
PARITY, TILE_LO, TILE_HI, SHIFT_BASE, SLAB = range(5)
SMEM = pl.BlockSpec(memory_space=pltpu.SMEM)
VMEM = pl.BlockSpec(memory_space=pltpu.VMEM)
PARAMS = pltpu.CompilerParams(vmem_limit_bytes=24 * 2**20)


def lanes_at(start):
    return pl.ds(pl.multiple_of(start, LANES), LANES)


def volume_lane(block, blocks, which):
    per = blocks // 2
    slab = block // per
    return ((2 * slab + which) * per + block - slab * per) * LANES


def lift_blocks(shift, halo):
    return jnp.maximum(halo - shift + SUB - 1, 0) // SUB


def sink_blocks(shift, halo):
    return jnp.maximum(shift - halo + SUB - 1, 0) // SUB


def slot(start, j, room):
    return jnp.minimum(start + j, room)


def room_for(slices, halo):
    usual = slices + 4 * math.sqrt(slices)
    return min(slices * (halo // SUB), int(usual))


def fits_kernel(chunks, halo, shifts, out):
    shift = shifts[...]
    total = shift.shape[1]
    index = lax.broadcasted_iota(jnp.int32, shift.shape, 1)
    lift = jnp.maximum(halo - shift + SUB - 1, 0) // SUB
    sink = jnp.maximum(shift - halo + SUB - 1, 0) // SUB
    excess = jnp.zeros((1, 1), jnp.int32)
    start = 0
    while start < total:
        for chunk in chunks:
            inside = (index >= start) & (index < start + chunk)
            room = room_for(chunk, halo)
            for need in (lift, sink):
                count = jnp.sum(jnp.where(inside, need, 0).astype(jnp.float32), axis=1, keepdims=True)
                excess = jnp.maximum(excess, count.astype(jnp.int32) - room)
            start += chunk
    out[...] = excess


def fits(shifts, chunks, halo):
    excess = pl.pallas_call(
        functools.partial(fits_kernel, chunks, halo),
        out_shape=jax.ShapeDtypeStruct((1, 1), jnp.int32),
        in_specs=[VMEM],
        out_specs=VMEM,
        name="fits",
    )(shifts.reshape(1, -1))
    return excess[0, 0] <= 0


def compose_kernel(first, last, part, packed, chunk_start, slices, rows, halo, inv_depth, unroll,
                   meta, shifts, sign_own, centers, widths, extinct, colors,
                   volume, recv, below, above, *rest):
    if first:
        state_in, (out, scratch) = None, rest
    else:
        state_in, out, scratch = rest
    lobes = centers.shape[0]
    band = 2 * rows
    room = above.shape[0] - 1
    filled = halo + band + halo
    tail = scratch.shape[2] - filled
    parity, tile_lo, tile_hi = meta[PARITY], meta[TILE_LO], meta[TILE_HI]
    shift_base = meta[SHIFT_BASE] + chunk_start
    at_own = pl.multiple_of(halo + parity * rows, SUB)
    at_recv = pl.multiple_of(halo + rows - parity * rows, SUB)
    blocks = recv.shape[-1] // LANES

    def splat(v):
        return jnp.full((SUB, LANES), v, jnp.float32)

    gain = [splat(extinct[k]) * (LOG2E * inv_depth) for k in range(lobes)]
    slope = [jnp.sqrt(splat(widths[k]) * LOG2E) for k in range(lobes)]
    offset = [slope[k] * splat(centers[k]) for k in range(lobes)]
    level = [jnp.log(gain[k]) * LOG2E for k in range(lobes)]

    count = scratch.shape[0]
    if part is None:
        base = jnp.int32(0)
    else:
        base = (meta[SLAB] if part else 1 - meta[SLAB]) * count
    cols_of = [lanes_at((base + b) * LANES) for b in range(count)]
    own_of = [lanes_at(volume_lane(base + b, blocks, parity)) for b in range(count)]

    def fill(s, carry):
        lift, sink = carry
        shift = shifts[shift_base + s]
        for j in range(halo // SUB):
            low, high = slot(lift, j, room), slot(sink, j, room)
            to_low, to_high = halo - (j + 1) * SUB, halo + band + j * SUB
            for b in range(count):
                if packed:
                    scratch[b, s, to_low:to_low + SUB, :] = below[low, :, cols_of[b]].astype(jnp.float32)
                    scratch[b, s, to_high:to_high + SUB, :] = above[high, :, cols_of[b]].astype(jnp.float32)
        for b in range(count):
            scratch[b, s, filled:, :] = jnp.zeros((tail, LANES), jnp.float32)
            scratch[b, s, pl.ds(at_own, rows), :] = volume[chunk_start + s, :, own_of[b]].astype(jnp.float32)
            scratch[b, s, pl.ds(at_recv, rows), :] = recv[s, :, cols_of[b]].astype(jnp.float32)
            if not packed:
                scratch[b, s, 0:halo, :] = below[s, :, cols_of[b]].astype(jnp.float32)
                scratch[b, s, halo + band:filled, :] = above[s, :, cols_of[b]].astype(jnp.float32)
        return lift + lift_blocks(shift, halo), sink + sink_blocks(shift, halo)

    lax.fori_loop(0, slices, fill, (jnp.int32(0), jnp.int32(0)))
    if first:
        for b in range(count):
            if packed:
                for j in range(halo // SUB):
                    to = halo - (j + 1) * SUB
                    scratch[b, slices, to:to + SUB, :] = below[room + 1 + j, :, cols_of[b]].astype(jnp.float32)
            else:
                scratch[b, slices, 0:halo, :] = below[slices, :, cols_of[b]].astype(jnp.float32)
            scratch[b, slices, pl.ds(at_own, rows), :] = jnp.full((rows, LANES), sign_own[0], jnp.float32)
            scratch[b, slices, pl.ds(at_recv, rows), :] = recv[slices, :, cols_of[b]].astype(jnp.float32)

    def column(block, carry):
        cols = lanes_at((base + block) * LANES)
        here_cols = lanes_at(block * LANES)

        def tile(t, carry):
            row = pl.multiple_of(t * SUB, SUB)
            here = pl.ds(row, SUB)
            if first:
                sign = scratch[block, slices, here, :]
                depth = jnp.zeros((SUB, LANES), jnp.float32)
                acc = [jnp.zeros((SUB, LANES), jnp.float32) for _ in range(lobes)]
            else:
                sign = state_in[lobes + 1, here, cols]
                depth = state_in[lobes, here, cols]
                acc = [state_in[k, here, cols] for k in range(lobes)]
            trans = jnp.exp2(depth * sign)

            def body(j, c):
                depth, trans, acc = c
                for u in range(unroll):
                    s = j * unroll + u
                    x = scratch[block, s, pl.ds(shifts[shift_base + s] + row, SUB), :]
                    lobe = []
                    optical = None
                    for k in range(lobes):
                        t_k = x * slope[k] - offset[k]
                        e = jnp.exp2(level[k] - t_k * t_k)
                        lobe.append(e)
                        optical = e if optical is None else optical + e
                    depth = depth + optical
                    new = jnp.exp2(depth * sign)
                    step = new - trans
                    acc = [acc[k] + step * lobe[k] for k in range(lobes)]
                    trans = new
                return depth, trans, acc

            depth, trans, acc = lax.fori_loop(0, slices // unroll, body, (depth, trans, acc))
            if last:
                norm = jnp.where(sign < 0, splat(-1.0), 1.0 / trans)
                for c in range(colors.shape[0]):
                    total = None
                    for k in range(lobes):
                        term = acc[k] * (splat(colors[c, k]) / gain[k])
                        total = term if total is None else total + term
                    out[c, here, here_cols] = total * norm
                out[CHANNELS - 1, here, here_cols] = depth * LN2
                out[CHANNELS, here, here_cols] = sign
            else:
                for k in range(lobes):
                    out[k, here, here_cols] = acc[k]
                out[lobes, here, here_cols] = depth
                out[lobes + 1, here, here_cols] = sign
            return carry

        lax.fori_loop(tile_lo, tile_hi, tile, 0)
        return carry

    lax.fori_loop(0, count, column, 0)


def compose(meta, shifts, sign_own, params, volume, recv, below, above, state,
            *, first, last, part, packed, chunk_start, slices, inv_depth, unroll):
    rows = volume.shape[1]
    halo = 3 * rows // 2
    band = 2 * rows
    cols = recv.shape[2]
    out_rows = band + halo
    lobes = params[0].shape[0]
    args = [meta, shifts, sign_own, *params, volume, recv, below, above]
    specs = [SMEM] * 7 + [VMEM] * 4
    aliases = {}
    if not first:
        args.append(state)
        specs.append(VMEM)
        if not last:
            aliases = {len(args) - 1: 0}
    n_out = CHANNELS + 1 if last else lobes + 2
    out_cols = cols if part is None else cols // 2
    samples = slices * out_rows * out_cols
    return pl.pallas_call(
        functools.partial(compose_kernel, first, last, part, packed, chunk_start, slices, rows, halo, inv_depth, unroll),
        out_shape=jax.ShapeDtypeStruct((n_out, out_rows, out_cols), jnp.float32),
        in_specs=specs,
        out_specs=VMEM,
        scratch_shapes=[pltpu.VMEM(
            (out_cols // LANES, slices + (1 if first else 0), filled_rows(rows, halo), LANES), jnp.float32)],
        input_output_aliases=aliases,
        compiler_params=PARAMS,
        cost_estimate=pl.CostEstimate(flops=samples * 60, transcendentals=samples * 9, bytes_accessed=samples * 3),
        name="compose_first" if first else "compose_last" if last else "compose_mid",
    )(*args)


def filled_rows(rows, halo):
    return 2 * rows + 3 * halo


def split_kernel(slices, chunk_start, meta, sign_own, volume, out):
    blocks = out.shape[2] // LANES
    other = 1 - meta[PARITY]
    for b in range(blocks):
        source = lanes_at(volume_lane(b, blocks, other))
        out[0:slices, :, b * LANES:(b + 1) * LANES] = volume[chunk_start:chunk_start + slices, :, source]
    if out.shape[0] > slices:
        sign = jnp.full((out.shape[1], out.shape[2]), sign_own[0], jnp.float32)
        out[slices] = sign.astype(out.dtype)


def split_first_kernel(slices, meta, sign_own, volume, out, done):
    half = out.shape[2] // 2
    other = 1 - meta[PARITY]
    sign = jnp.full((out.shape[1], out.shape[2]), sign_own[0], jnp.float32)
    out[slices] = sign.astype(out.dtype)
    copies = [
        pltpu.make_async_copy(
            volume.at[0:slices, :, pl.ds(pl.multiple_of((2 * s + other) * half, LANES), half)],
            out.at[0:slices, :, s * half:(s + 1) * half],
            done.at[s])
        for s in range(2)
    ]
    for copy in copies:
        copy.start()
    for copy in copies:
        copy.wait()


def split(meta, sign_own, volume, chunk_start, slices, first):
    rows, cols = volume.shape[1], volume.shape[2]
    total = slices + (1 if first else 0)
    if first:
        return pl.pallas_call(
            functools.partial(split_first_kernel, slices),
            out_shape=jax.ShapeDtypeStruct((total, rows, cols // 2), volume.dtype),
            in_specs=[SMEM, SMEM, pl.BlockSpec(memory_space=pl.ANY)],
            out_specs=VMEM,
            scratch_shapes=[pltpu.SemaphoreType.DMA((2,))],
            compiler_params=PARAMS,
            cost_estimate=pl.CostEstimate(flops=0, transcendentals=0, bytes_accessed=2 * total * rows * cols),
            name="split_first",
        )(meta, sign_own, volume)
    return pl.pallas_call(
        functools.partial(split_kernel, slices, chunk_start),
        out_shape=jax.ShapeDtypeStruct((total, rows, cols // 2), volume.dtype),
        in_specs=[SMEM, SMEM, VMEM],
        out_specs=VMEM,
        compiler_params=PARAMS,
        cost_estimate=pl.CostEstimate(flops=0, transcendentals=0, bytes_accessed=2 * total * rows * cols),
        name="split",
    )(meta, sign_own, volume)


def pack_kernel(slices, chunk_start, rows, halo, meta, sign_own, volume, recv, upper, lower):
    blocks = recv.shape[2] // LANES
    odd_in_upper = halo - rows
    even_from = 2 * rows - halo
    flags = recv.shape[0] > slices
    parity = meta[PARITY]

    def place(own_is_even):
        for b in range(blocks):
            cols = slice(b * LANES, (b + 1) * LANES)
            source = lanes_at(volume_lane(b, blocks, parity))

            def one(s, carry):
                own = volume[chunk_start + s, :, source]
                other = recv[s, :, cols]
                even, odd = (own, other) if own_is_even else (other, own)
                upper[s, 0:rows, cols] = even
                upper[s, rows:halo, cols] = odd[0:odd_in_upper]
                lower[s, 0:halo - rows, cols] = even[even_from:rows]
                lower[s, halo - rows:halo, cols] = odd
                return carry

            lax.fori_loop(0, slices, one, 0, unroll=4)
        if flags:
            own = jnp.full((rows, lower.shape[2]), sign_own[0], jnp.float32).astype(lower.dtype)
            other = recv[slices]
            even, odd = (own, other) if own_is_even else (other, own)
            lower[slices, 0:halo - rows, :] = even[even_from:rows]
            lower[slices, halo - rows:halo, :] = odd

    @pl.when(parity == 0)
    def _():
        place(True)

    @pl.when(parity == 1)
    def _():
        place(False)


def pack(meta, sign_own, volume, recv, chunk_start, slices, halo):
    rows = volume.shape[1]
    total, _, cols = recv.shape
    return pl.pallas_call(
        functools.partial(pack_kernel, slices, chunk_start, rows, halo),
        out_shape=[
            jax.ShapeDtypeStruct((slices, halo, cols), recv.dtype),
            jax.ShapeDtypeStruct((total, halo, cols), recv.dtype),
        ],
        in_specs=[SMEM, SMEM, VMEM, VMEM],
        out_specs=[VMEM, VMEM],
        compiler_params=PARAMS,
        cost_estimate=pl.CostEstimate(flops=0, transcendentals=0, bytes_accessed=4 * total * rows * cols),
        name="pack",
    )(meta, sign_own, volume, recv)


def pack_blocks_kernel(slices, chunk_start, rows, halo, flags, meta, shifts, sign_own, volume, recv, upper, lower):
    blocks = recv.shape[2] // LANES
    parity = meta[PARITY]
    shift_base = meta[SHIFT_BASE] + chunk_start
    room = upper.shape[0] - 1

    def place(own_is_even):
        def one(s, carry):
            lift, sink = carry
            shift = shifts[shift_base + s]
            for b in range(blocks):
                cols = slice(b * LANES, (b + 1) * LANES)
                own = volume[chunk_start + s, :, lanes_at(volume_lane(b, blocks, parity))]
                other = recv[s, :, cols]
                even, odd = (own, other) if own_is_even else (other, own)
                pieces = [x[r:r + SUB] for x in (even, odd) for r in range(0, rows, SUB)]
                for j in range(halo // SUB):
                    upper[slot(sink, j, room), :, cols] = pieces[j]
                    lower[slot(lift, j, room), :, cols] = pieces[-1 - j]
            return lift + lift_blocks(shift, halo), sink + sink_blocks(shift, halo)

        lax.fori_loop(0, slices, one, (jnp.int32(0), jnp.int32(0)), unroll=2)
        if flags:
            own = jnp.full((rows, lower.shape[2]), sign_own[0], jnp.float32).astype(lower.dtype)
            other = recv[slices]
            even, odd = (own, other) if own_is_even else (other, own)
            pieces = [x[r:r + SUB] for x in (even, odd) for r in range(0, rows, SUB)]
            for j in range(halo // SUB):
                lower[room + 1 + j] = pieces[-1 - j]

    @pl.when(parity == 0)
    def _():
        place(True)

    @pl.when(parity == 1)
    def _():
        place(False)


def pack_blocks(meta, shifts, sign_own, volume, recv, chunk_start, slices, halo):
    rows = volume.shape[1]
    total, _, cols = recv.shape
    flags = total > slices
    slots = room_for(slices, halo) + 1
    return pl.pallas_call(
        functools.partial(pack_blocks_kernel, slices, chunk_start, rows, halo, flags),
        out_shape=[
            jax.ShapeDtypeStruct((slots, SUB, cols), recv.dtype),
            jax.ShapeDtypeStruct((slots + (halo // SUB if flags else 0), SUB, cols), recv.dtype),
        ],
        in_specs=[SMEM, SMEM, SMEM, VMEM, VMEM],
        out_specs=[VMEM, VMEM],
        compiler_params=PARAMS,
        cost_estimate=pl.CostEstimate(flops=0, transcendentals=0, bytes_accessed=4 * total * rows * cols),
        name="pack_blocks",
    )(meta, shifts, sign_own, volume, recv)


def merge_kernel(rows, lead, meta, mine, got, here, side, up, cross, image):
    parity, slab = meta[PARITY], meta[SLAB]
    band = 2 * rows
    blocks = mine.shape[2] // LANES
    image[:, 0:lead, :] = jnp.zeros((CHANNELS, lead, LANES), jnp.float32)
    for b in range(blocks):
        cols = slice(b * LANES, (b + 1) * LANES)
        a_sum, b_sum = mine[CHANNELS - 1, :, cols], got[CHANNELS - 1, :, cols]
        first = jnp.where(slab == 0, -1.0, 1.0) * mine[CHANNELS, :, cols] > 0
        through = jnp.exp(-jnp.where(first, a_sum, b_sum))
        for c in range(CHANNELS - 1):
            a, g = mine[c, :, cols], got[c, :, cols]
            image[c, lead:, :] = jnp.where(first, a, g) + through * jnp.where(first, g, a)
        image[CHANNELS - 1, lead:, :] = 1.0 - jnp.exp(-(a_sum + b_sum))

        def rows_at(start):
            return image[:, pl.ds(pl.multiple_of(start, SUB), rows), :]

        here[:, :, cols] = rows_at(band + rows * parity)
        side[:, :, cols] = rows_at(band + rows - rows * parity)
        up[:, :, cols] = rows_at(rows * parity)
        cross[:, :, cols] = rows_at(rows - rows * parity)


def merge(meta, mine, got, rows, lead):
    out_rows, cols = mine.shape[1:]
    shape = jax.ShapeDtypeStruct((CHANNELS, rows, cols), jnp.float32)
    return pl.pallas_call(
        functools.partial(merge_kernel, rows, lead),
        out_shape=[shape] * 4,
        in_specs=[SMEM, VMEM, VMEM],
        out_specs=[VMEM] * 4,
        scratch_shapes=[pltpu.VMEM((CHANNELS, lead + out_rows, LANES), jnp.float32)],
        compiler_params=PARAMS,
        name="merge",
    )(meta, mine, got)


CHUNKS = (4, 4, 5, 3)


def chunk_sizes(slice_count):
    return [slice_count * part // sum(CHUNKS) for part in CHUNKS]


def unroll_of(chunk):
    return max(u for u in range(1, 17) if chunk % u == 0)


def render(packed, volume, shift_table, slab_order, centers, widths, extinct, colors):
    slab_count = lax.axis_size("depth")
    slab = lax.axis_index("depth")
    n = lax.axis_size("lat")
    me = lax.axis_index("lat")
    pair, parity = me // 2, me % 2
    slice_count, rows, _ = volume.shape
    band = 2 * rows
    halo = 3 * rows // 2
    inv_depth = 1.0 / (slice_count * slab_count)
    swap = [(i, i ^ 1) for i in range(n)]
    down = [(i, i - 2) for i in range(2, n)]
    up = [(i - 2, i) for i in range(2, n)]
    cross = [(i, (i ^ 1) - 2) for i in range(2, n)]
    is_last = pair == n // 2 - 1
    meta = jnp.stack([
        parity,
        jnp.where(pair == 0, halo // SUB, 0),
        jnp.where(is_last, (band + halo) // SUB, band // SUB),
        slab * slice_count,
        slab,
    ]).astype(jnp.int32)
    sign_own = jnp.where(slab_order[:, 0] == 0, -1.0, 1.0)
    params = (centers, widths, extinct, colors)

    state = None
    start = 0
    for c, chunk in enumerate(chunk_sizes(slice_count)):
        first, last = c == 0, c == len(CHUNKS) - 1
        give = split(meta, sign_own, volume, start, chunk, first)
        recv = lax.ppermute(give, "lat", swap)
        if packed:
            upper, lower = pack_blocks(meta, shift_table, sign_own, volume, recv, start, chunk, halo)
        else:
            upper, lower = pack(meta, sign_own, volume, recv, start, chunk, halo)
        above = lax.ppermute(upper, "lat", down)
        below = lax.ppermute(lower, "lat", up)
        run = functools.partial(
            compose, meta, shift_table, sign_own, params, volume, recv, below, above, state,
            first=first, last=last, packed=packed, chunk_start=start, slices=chunk,
            inv_depth=inv_depth, unroll=unroll_of(chunk))
        if last:
            give = run(part=0)
            mine = run(part=1)
        else:
            state = run(part=None)
        start += chunk
    got = lax.ppermute(give, "depth", [(0, 1), (1, 0)])
    lead = band - halo
    from_pair, side, upper, diagonal = merge(meta, mine, got, rows, lead)
    from_side = lax.ppermute(side, "lat", swap)
    from_up = lax.ppermute(upper, "lat", down)
    from_cross = lax.ppermute(diagonal, "lat", cross)
    index = rows * parity + jnp.arange(rows)
    inside = (is_last | (index < lead))[None, :, None]
    a = jnp.where(inside, from_pair, from_up)
    b = jnp.where(inside, from_side, from_cross)
    return jnp.where(parity == 0, jnp.concatenate([a, b], axis=2), jnp.concatenate([b, a], axis=2))


def local(volume, shift_table, *rest):
    halo = 3 * volume.shape[1] // 2
    usual = fits(shift_table, chunk_sizes(volume.shape[0]), halo)

    def branch(packed):
        def run(*args):
            return render(packed, *args)

        return run

    return lax.cond(usual, branch(True), branch(False), volume, shift_table, *rest)


def solution(mesh):
    in_specs = (
        P(("views", "depth"), "lat", None),
        P("views"),
        P(("views", "lat"), None),
        P(),
        P(),
        P(),
        P(),
    )
    out_specs = P(None, ("views", "lat"), "depth")
    return jax.shard_map(local, mesh=mesh, in_specs=in_specs, out_specs=out_specs, check_vma=False)
```
